32 devices in a mesh: req: 16 (over z, y, x), head: 2 (over core).
Axes of the slice: x: 2, y: 2, z: 4, core: 2. Of those that a mesh axis runs over, the one named last changes fastest.
Arguments:
- queries: bfloat16 [8192, 8192], P('req', 'head'), may hold values from -8 to 8
- keys_values: bfloat16 [8192, 2048], P('req', 'head'), may hold values from -8 to 8
- seg_ids: int32 [8192], replicated, may hold values from -1 to 13, as said below
- cache_page: int32 [512], replicated, may hold values from 0 to 511, as said below
Outputs:
- context: bfloat16 [8192, 8192], P('req', 'head')
- cache: bfloat16 [8192, 2048], P('req', 'head')
The draws below stay inside these ranges and needn't reach their ends.
Inputs may be any that keep to these rules, and one draw needn't show every extreme that they name: `seg_ids`: stream s occupies the 4096 positions that start at s * 4096 + 256, counted modulo 8192: first its shared prompt (id s * 7, at least one token), then its 6 requests in order (ids s * 7 + 1 to s * 7 + 6, each at least one token), then padding: 1 to 255 tokens in every stream but the last, and 256 to 512 tokens in the last, so that positions 0 to 255 are padding. `cache_page`: every cache page is named once. Cache pages d * 32 to d * 32 + 31 belong to index d of req; the 32 token pages of one index of req go to exactly 16 owners, exactly 2 pages to each.
All inputs are finite; a program needn't handle non-finite values.
Results may differ from the reference program's by a relative error of at most 0.0055.
Values may be sent and summed in bfloat16 or wider, within the bound.
A program may use at most 128 MiB of HBM per device.

```python
import jax
import jax.numpy as jnp
from jax import lax

QH = 64
KVH = 8
HD = 128
STREAM = 4096
REQS = 6
PAGE = 16
TOKENS = 8192
NPAGES = 512
PG_DEV = 32
CAP = 2
LEAD = 256
N_REQ = 16


def draw_queries(key, part):
    shape = (TOKENS, KVH, QH // KVH, HD)
    own_key = jax.random.fold_in(key, 1)
    values = jnp.clip(jax.random.normal(own_key, shape, jnp.float32), -6.0, 6.0)
    return values.reshape(TOKENS, QH * HD).astype(jnp.bfloat16)


def draw_keys_values(key, part):
    shape = (TOKENS, KVH, 2, HD)
    own_key = jax.random.fold_in(key, 2)
    values = jnp.clip(jax.random.normal(own_key, shape, jnp.float32), -6.0, 6.0)
    return values.reshape(TOKENS, KVH * 2 * HD).astype(jnp.bfloat16)


def draw_seg_ids(key, part):
    streams = TOKENS // STREAM

    def one_stream(stream_key, stream_index):
        key_pre, key_pad, key_last, key_share = jax.random.split(stream_key, 4)
        prefix = jax.random.randint(key_pre, (), STREAM // 16, STREAM // 4 + 1)
        drawn_pad = jax.random.randint(key_pad, (), 1, STREAM // 16)
        last_pad = jax.random.randint(key_last, (), LEAD, STREAM // 8 + 1)
        padding = jnp.where(stream_index == streams - 1, last_pad, drawn_pad)
        shares = jax.random.randint(key_share, (REQS,), 1, 9)
        running = jnp.cumsum(shares)
        remainder = STREAM - prefix - padding
        bounds = remainder * running[:-1] // running[-1]
        position = jnp.arange(STREAM, dtype=jnp.int32)
        offset = position - prefix
        local_id = 1 + jnp.sum((offset[:, None] >= bounds[None, :]).astype(jnp.int32), axis=1)
        local_id = jnp.where(position < prefix, 0, local_id)
        local_id = jnp.where(position >= prefix + remainder, -1, local_id)
        return jnp.where(local_id >= 0, stream_index * (REQS + 1) + local_id, -1).astype(jnp.int32)
    stream_keys = jax.random.split(key, streams)
    laid = jax.vmap(one_stream)(stream_keys, jnp.arange(streams, dtype=jnp.int32)).reshape(-1)
    return jnp.roll(laid, LEAD, axis=0)


def draw_cache_page(key, part):
    rounds = PG_DEV // CAP
    key_rho, key_sigma, key_offs, key_pis, key_taus = jax.random.split(key, 5)
    owner_perm = jax.random.permutation(key_rho, N_REQ)
    source_perm = jax.random.permutation(key_sigma, N_REQ)
    offsets = jax.random.permutation(key_offs, N_REQ)[:rounds]
    page_perms = jax.vmap(lambda one_key: jax.random.permutation(one_key, PG_DEV))(jax.random.split(key_pis, N_REQ))
    slot_perms = jax.vmap(lambda one_key: jax.random.permutation(one_key, PG_DEV))(jax.random.split(key_taus, N_REQ))
    round_of = page_perms // CAP
    within = page_perms % CAP
    owners = owner_perm[(source_perm[:, None] + offsets[round_of]) % N_REQ]
    slots = slot_perms[owners, round_of * CAP + within]
    return (owners * PG_DEV + slots).reshape(-1).astype(jnp.int32)


def setup_inputs(seed: int = 0) -> dict:
    key_of = jax.random.split(jax.random.key(seed), 5)
    queries = draw_queries(jax.random.fold_in(key_of[4], 71), 0)
    keys_values = draw_keys_values(jax.random.fold_in(key_of[4], 71), 0)
    seg_ids = draw_seg_ids(jax.random.fold_in(key_of[4], 71), 0)
    cache_page = draw_cache_page(jax.random.fold_in(key_of[4], 71), 0)
    return dict(queries=queries, keys_values=keys_values, seg_ids=seg_ids, cache_page=cache_page)


NEG_FILL = -1e+30

def reference(queries, keys_values, seg_ids, cache_page):
    streams = TOKENS // STREAM
    per_group = QH // KVH
    score_scale = 1.0 / jnp.sqrt(jnp.float32(HD))
    rolled_q = jnp.roll(queries, -LEAD, axis=0)
    rolled_kv = jnp.roll(keys_values, -LEAD, axis=0)
    rolled_seg = jnp.roll(seg_ids, -LEAD, axis=0)
    query_split = rolled_q.reshape(streams, STREAM, KVH, per_group, HD)
    pair_split = rolled_kv.reshape(streams, STREAM, KVH, 2, HD)
    seg_split = rolled_seg.reshape(streams, STREAM)
    position = jnp.arange(STREAM, dtype=jnp.int32)

    def per_stream(item):
        stream_q, stream_kv, stream_seg = item
        shared = stream_seg // (REQS + 1) * (REQS + 1)
        is_live = stream_seg >= 0
        visible = is_live[:, None] & (stream_seg[None, :] >= 0) & (position[None, :] <= position[:, None])
        visible = visible & ((stream_seg[None, :] == stream_seg[:, None]) | (stream_seg[None, :] == shared[:, None]))

        def per_head(head_item):
            head_q, head_k, head_v = head_item
            scores = jnp.einsum('qrd,kd->rqk', head_q.astype(jnp.float32), head_k.astype(jnp.float32)) * score_scale
            scores = jnp.where(visible[None], scores, NEG_FILL)
            row_top = lax.optimization_barrier(jnp.max(scores, axis=-1))
            weight = jnp.where(visible[None], jnp.exp(scores - row_top[..., None]), 0.0)
            row_total = lax.optimization_barrier(jnp.sum(weight, axis=-1))
            weight_low = lax.optimization_barrier(weight.astype(jnp.bfloat16)).astype(jnp.float32)
            weighted = jnp.einsum('rqk,kd->rqd', weight_low, head_v.astype(jnp.float32))
            safe_total = jnp.where(is_live[None, :], row_total, 1.0)
            return jnp.where(is_live[None, :, None], weighted / safe_total[..., None], 0.0)
        heads_out = lax.map(per_head, (jnp.transpose(stream_q, (1, 0, 2, 3)), jnp.transpose(stream_kv[:, :, 0, :], (1, 0, 2)), jnp.transpose(stream_kv[:, :, 1, :], (1, 0, 2))))
        return jnp.transpose(heads_out, (2, 0, 1, 3)).reshape(STREAM, QH * HD)
    context = lax.map(per_stream, (query_split, pair_split, seg_split)).reshape(TOKENS, QH * HD).astype(jnp.bfloat16)
    context = jnp.roll(context, LEAD, axis=0)
    live_rows = (seg_ids >= 0)[:, None]
    masked = jnp.where(live_rows, keys_values, jnp.zeros_like(keys_values)).reshape(NPAGES, PAGE, KVH * 2 * HD)
    cache = jnp.zeros_like(masked).at[cache_page].set(masked).reshape(TOKENS, KVH * 2 * HD)
    return (context, cache)
```

```python
import functools
import math

import jax
import jax.numpy as jnp
from jax import lax
from jax.experimental import pallas as pl
from jax.experimental.pallas import tpu as pltpu
from jax.sharding import PartitionSpec as P

HD = 128
STREAM = 4096
REQS = 6
PAGE = 16

NEG_FILL = -1e30
TILE_Q = 128
TILE_K = 512
CHUNK_HEADS = 4
NEAR = 2
PROMPT_SHARDS = 3


def stream_pairs(count, group, offset, sources):
    return [
        (base + a, base + a + offset)
        for base in range(0, count, group)
        for a in sources
        if a + offset <= group and base + a + offset < count
    ]


def gather_window(keys_values, group, sparse):
    count = lax.axis_size("req")
    pieces = []
    for offset in range(1, group + 1):
        wide = not sparse or offset <= NEAR
        sources = range(group) if wide else range(min(PROMPT_SHARDS, group))
        pairs = stream_pairs(count, group, offset, sources)
        pieces.append(
            lax.ppermute(keys_values, "req", pairs) if pairs else jnp.zeros_like(keys_values)
        )
    return tuple(pieces)


def attend_kernel(
    pieces, tile_k, per_group, counts, blocks, kinds, info_ref, first_ref, q_ref, *refs
):
    kv_refs = refs[:pieces]
    out_ref, kv, stacked, top, acc = refs[pieces:]
    tile = pl.program_id(1)
    tile_q = q_ref.shape[0]
    shard_rows = kv_refs[0].shape[0]
    factor = math.log2(math.e) / math.sqrt(HD)

    @pl.when(tile == 0)
    def _():
        for index, ref in enumerate(kv_refs):
            kv[pl.ds(index * shard_rows, shard_rows), :] = ref[...]

    for head in range(per_group):
        stacked[pl.ds(head * tile_q, tile_q), :] = q_ref[:, head * HD : (head + 1) * HD]
    top[...] = jnp.full_like(top, NEG_FILL)
    acc[...] = jnp.zeros_like(acc)
    begin = info_ref[:, 0:1]
    stop = info_ref[:, 1:2]
    own = info_ref[:, 2:3]
    row = info_ref[:, 3:4]
    first_row = first_ref[0]
    ones = jnp.ones((tile_k, HD), jnp.bfloat16)

    def block(slot, masked):
        start = pl.multiple_of(blocks[tile, slot] * tile_k, tile_k)
        key = kv[pl.ds(start, tile_k), 0:HD]
        value = jnp.concatenate([kv[pl.ds(start, tile_k), HD : 2 * HD], ones], axis=1)
        if masked:
            at = first_row + start + lax.broadcasted_iota(jnp.int32, (tile_q, tile_k), 1)
            seen = (at <= row) & ((at >= own) | ((at >= begin) & (at < stop)))
            bias = jnp.where(seen, 0.0, NEG_FILL).astype(jnp.float32)
        chunk = min(CHUNK_HEADS, per_group)
        rows = chunk * tile_q
        for part in range(per_group // chunk):
            span = pl.ds(part * rows, rows)
            score = lax.dot_general(
                stacked[span, :], key, (((1,), (1,)), ((), ())),
                preferred_element_type=jnp.float32,
            )
            if masked:
                score = (score.reshape(chunk, tile_q, tile_k) + bias[None]).reshape(rows, tile_k)
            old = top[span, :]
            new = jnp.maximum(old, jnp.max(score, axis=1, keepdims=True))
            rescale = jnp.exp2((old - new) * factor)
            weight = jnp.exp2((score - jnp.tile(new, (1, tile_k // HD))) * factor)
            acc[span, :] = acc[span, :] * jnp.tile(rescale, (1, 2)) + jnp.dot(
                weight.astype(jnp.bfloat16), value, preferred_element_type=jnp.float32
            )
            top[span, :] = new

    def step(slot, carry):
        @pl.when(kinds[tile, slot] == 1)
        def _():
            block(slot, True)

        @pl.when(kinds[tile, slot] == 2)
        def _():
            block(slot, False)

        return carry

    lax.fori_loop(0, counts[tile], step, 0)
    live = row >= own
    for head in range(per_group):
        span = pl.ds(head * tile_q, tile_q)
        total = jnp.where(live, acc[span, HD : 2 * HD], 1.0)
        context = jnp.where(live, acc[span, 0:HD] / total, 0.0)
        out_ref[:, head * HD : (head + 1) * HD] = context.astype(out_ref.dtype)


def attend(queries, pieces, info, first_row, key_heads, per_group):
    shard_rows = queries.shape[0]
    tile_q = min(TILE_Q, shard_rows)
    tile_k = min(TILE_K, shard_rows)
    span_rows = len(pieces) * shard_rows
    tiles = shard_rows // tile_q
    blocks = span_rows // tile_k
    low = (first_row + jnp.arange(blocks, dtype=jnp.int32) * tile_k)[None, :]
    high = low + tile_k
    begin, stop, own, row = (info[:, c : c + 1] for c in range(4))
    end = jnp.minimum(stop, row + 1)
    touched = ((low < end) & (high > begin)) | ((low <= row) & (high > own))
    whole = ((low >= begin) & (high <= end)) | ((low >= own) & (high <= row + 1))
    touched = jnp.any(touched.reshape(tiles, tile_q, blocks), axis=1)
    whole = jnp.all(whole.reshape(tiles, tile_q, blocks), axis=1)
    kind = jnp.where(touched, jnp.where(whole, 2, 1), 0).astype(jnp.int32)
    counts = jnp.sum(touched.astype(jnp.int32), axis=1)
    place = jnp.cumsum(touched.astype(jnp.int32), axis=1) - 1
    slots = jnp.arange(blocks, dtype=jnp.int32)
    pick = touched[:, None, :] & (place[:, None, :] == slots[None, :, None])
    table = jnp.sum(jnp.where(pick, slots[None, None, :], 0), axis=2)
    kinds = jnp.sum(jnp.where(pick, kind[:, None, :], 0), axis=2)
    wide = per_group * HD
    kernel = functools.partial(attend_kernel, len(pieces), tile_k, per_group)
    flops = 4 * shard_rows * key_heads * wide * 1536
    return pl.pallas_call(
        kernel,
        out_shape=jax.ShapeDtypeStruct(queries.shape, jnp.bfloat16),
        grid_spec=pltpu.PrefetchScalarGridSpec(
            num_scalar_prefetch=3,
            grid=(key_heads, tiles),
            in_specs=[
                pl.BlockSpec((tile_q, info.shape[1]), lambda g, t, *_: (t, 0)),
                pl.BlockSpec(memory_space=pltpu.SMEM),
                pl.BlockSpec((tile_q, wide), lambda g, t, *_: (t, g)),
            ]
            + [pl.BlockSpec((shard_rows, 2 * HD), lambda g, t, *_: (0, g)) for _ in pieces],
            out_specs=pl.BlockSpec((tile_q, wide), lambda g, t, *_: (t, g)),
            scratch_shapes=[
                pltpu.VMEM((span_rows, 2 * HD), jnp.bfloat16),
                pltpu.VMEM((per_group * tile_q, HD), jnp.bfloat16),
                pltpu.VMEM((per_group * tile_q, HD), jnp.float32),
                pltpu.VMEM((per_group * tile_q, 2 * HD), jnp.float32),
            ],
        ),
        compiler_params=pltpu.CompilerParams(vmem_limit_bytes=48 << 20),
        cost_estimate=pl.CostEstimate(
            flops=flops, bytes_accessed=4 * queries.size + 2 * span_rows * key_heads * 2 * HD,
            transcendentals=flops // (4 * HD),
        ),
        name="attend",
    )(counts, table, kinds, info, first_row.reshape(1), queries, *pieces)


def pick_kernel(pages, index, source_ref, out_ref):
    def move(slot, carry):
        source = pl.multiple_of(index[slot] * PAGE, PAGE)
        target = pl.multiple_of(slot * PAGE, PAGE)
        out_ref[pl.ds(target, PAGE), :] = source_ref[pl.ds(source, PAGE), :]
        return carry

    lax.fori_loop(0, pages, move, 0)


def pick_pages(source, index):
    pages = index.shape[0]
    width = source.shape[1]
    return pl.pallas_call(
        functools.partial(pick_kernel, pages),
        out_shape=jax.ShapeDtypeStruct((pages * PAGE, width), source.dtype),
        grid_spec=pltpu.PrefetchScalarGridSpec(
            num_scalar_prefetch=1,
            grid=(1,),
            in_specs=[pl.BlockSpec(source.shape, lambda i, *_: (0, 0))],
            out_specs=pl.BlockSpec((pages * PAGE, width), lambda i, *_: (0, 0)),
        ),
        cost_estimate=pl.CostEstimate(
            flops=0, bytes_accessed=2 * (source.size + pages * PAGE * width), transcendentals=0
        ),
        name="pick",
    )(index, source)


def write_pages(keys_values, is_live, cache_page, own_index, axis_size):
    page_count = keys_values.shape[0] // PAGE
    capacity = (page_count + axis_size - 1) // axis_size
    slot_count = axis_size * capacity
    all_pages = cache_page.shape[0]
    owners = cache_page // page_count
    by_source = owners.reshape(axis_size, page_count)
    page_iota = jnp.arange(page_count, dtype=jnp.int32)
    earlier = page_iota[None, :] < page_iota[:, None]
    same_owner = by_source[:, :, None] == by_source[:, None, :]
    rank = jnp.sum((same_owner & earlier[None]).astype(jnp.int32), axis=2)
    my_owner = lax.dynamic_index_in_dim(by_source, own_index, 0, keepdims=False)
    my_rank = lax.dynamic_index_in_dim(rank, own_index, 0, keepdims=False)
    target_slot = my_owner * capacity + my_rank
    slot_iota = jnp.arange(slot_count, dtype=jnp.int32)
    send_page = jnp.sum(
        jnp.where(slot_iota[:, None] == target_slot[None, :], page_iota[None, :], 0), axis=1
    )
    masked = jnp.where(is_live[:, None], keys_values, jnp.zeros_like(keys_values))
    outgoing = pick_pages(masked, send_page)
    incoming = lax.all_to_all(outgoing, "req", split_axis=0, concat_axis=0, tiled=True)
    wanted = own_index * page_count + page_iota
    hits = cache_page[None, :] == wanted[:, None]
    page_slot = jnp.arange(all_pages, dtype=jnp.int32) // page_count * capacity + rank.reshape(-1)
    arrival = jnp.sum(jnp.where(hits, page_slot[None, :], 0), axis=1)
    return pick_pages(incoming, arrival)


def on_device(queries, keys_values, seg_ids, cache_page):
    shard_rows = queries.shape[0]
    key_heads = keys_values.shape[1] // (2 * HD)
    per_group = queries.shape[1] // HD // key_heads
    tokens = seg_ids.shape[0]
    own_index = lax.axis_index("req")
    axis_size = lax.axis_size("req")
    group = STREAM // shard_rows

    ids = jnp.arange(tokens // STREAM * (REQS + 1), dtype=jnp.int32)
    position = jnp.arange(tokens, dtype=jnp.int32)
    member = seg_ids[None, :] == ids[:, None]
    starts = jnp.min(jnp.where(member, position[None, :], tokens), axis=1)
    stops = jnp.max(jnp.where(member, position[None, :], -1), axis=1) + 1

    query_rows = own_index * shard_rows + jnp.arange(shard_rows, dtype=jnp.int32)
    query_seg = lax.dynamic_slice_in_dim(seg_ids, own_index * shard_rows, shard_rows)
    is_live = query_seg >= 0
    shared = query_seg // (REQS + 1) * (REQS + 1)
    far = 2 * tokens
    is_shared = shared[:, None] == ids[None, :]
    is_own = query_seg[:, None] == ids[None, :]
    begin = jnp.sum(jnp.where(is_shared, starts[None, :], 0), axis=1)
    stop = jnp.sum(jnp.where(is_shared, stops[None, :], 0), axis=1)
    own = jnp.sum(jnp.where(is_own, starts[None, :], 0), axis=1)
    begin = jnp.where(is_live, begin, far)
    stop = jnp.where(is_live, stop, 0)
    own = jnp.where(is_live, own, far)
    zero = jnp.zeros_like(own)
    info = jnp.stack([begin, stop, own, query_rows, zero, zero, zero, zero], axis=1)

    stream_base = ids // (REQS + 1) * group
    is_prompt = ids % (REQS + 1) == 0
    last_shard = (stops - 1) // shard_rows
    prompt_ok = last_shard < stream_base + PROMPT_SHARDS
    request_ok = last_shard - starts // shard_rows <= NEAR
    short = jnp.all(jnp.where(is_prompt, prompt_ok, request_ok))
    window = lax.cond(
        short,
        lambda kv: gather_window(kv, group, True),
        lambda kv: gather_window(kv, group, False),
        keys_values,
    )
    pieces = tuple(window[::-1]) + (keys_values,)
    first_row = ((own_index - group) * shard_rows).astype(jnp.int32)
    context = attend(queries, pieces, info, first_row, key_heads, per_group)
    cache = write_pages(keys_values, is_live, cache_page, own_index, axis_size)
    return (context, cache)


def solution(mesh):
    return jax.shard_map(
        on_device,
        mesh=mesh,
        in_specs=(P("req", "head"), P("req", "head"), P(), P()),
        out_specs=(P("req", "head"), P("req", "head")),
        check_vma=False,
    )
```

```python
import functools
import math

import jax
import jax.numpy as jnp
from jax import lax
from jax.experimental import pallas as pl
from jax.experimental.pallas import tpu as pltpu
from jax.sharding import PartitionSpec as P

HD = 128
STREAM = 4096
REQS = 6
PAGE = 16

NEG_FILL = -1e30
TILE_Q = 128
TILE_K = 256
CHUNK_HEADS = 4
NEAR = 2
CHUNK = 256
LEAD = 256
ROUNDS = (
    ((0, 5, 0), (1, 6, 1), (2, 7, 2), (4, 8, 3), (3, 4, 1)),
    ((0, 6, 0), (1, 7, 1), (4, 5, 3), (3, 8, 2), (2, 4, 0)),
    ((0, 7, 0), (1, 8, 1), (2, 5, 2), (4, 6, 3), (3, 4, 2)),
    ((0, 8, 0), (1, 5, 1), (3, 6, 2), (4, 7, 3), (2, 3, 0)),
)


def from_before(keys_values, group, offset):
    count = lax.axis_size("req")
    pairs = [
        (base + a, base + a + offset)
        for base in range(0, count, group)
        for a in range(group)
        if a + offset <= group and base + a + offset < count
    ]
    return lax.ppermute(keys_values, "req", pairs) if pairs else jnp.zeros_like(keys_values)


def full_window(keys_values, group, own_index, tokens):
    shard_rows = keys_values.shape[0]
    pieces = [from_before(keys_values, group, offset) for offset in range(group, 0, -1)]
    blocks = (group + 1) * shard_rows // TILE_K
    first = (own_index - group) * shard_rows
    return pieces + [keys_values], first + jnp.arange(blocks, dtype=jnp.int32) * TILE_K


def short_window(keys_values, group, own_index, tokens):
    count = lax.axis_size("req")
    shard_rows = keys_values.shape[0]
    near = [from_before(keys_values, group, offset) for offset in range(NEAR, 0, -1)]
    pieces = near + [keys_values]
    held = jnp.concatenate(pieces, axis=0)
    blocks = held.shape[0] // TILE_K
    first = (own_index - NEAR) * shard_rows
    lows = [first + jnp.arange(blocks, dtype=jnp.int32) * TILE_K]
    place = own_index % group
    target_place = jnp.where(place == 0, group, place)
    base_row = (own_index - target_place) * shard_rows + LEAD
    for sends in ROUNDS:
        send = jnp.int32(0)
        take = jnp.int32(-1)
        for source, target, chunk in sends:
            row = LEAD + chunk * CHUNK - (source - NEAR) * shard_rows
            send = jnp.where(place == source, row, send)
            take = jnp.where(target_place == target, chunk, take)
        pairs = [
            (base + source, base + target)
            for base in range(0, count, group)
            for source, target, _ in sends
            if base + target < count
        ]
        pieces.append(
            lax.ppermute(lax.dynamic_slice_in_dim(held, send, CHUNK, 0), "req", pairs)
        )
        lows.append(jnp.where(take >= 0, base_row + take * CHUNK, 2 * tokens)[None])
    return pieces, jnp.concatenate(lows).astype(jnp.int32)


def attend_kernel(
    pieces, tile_k, per_group, counts, blocks, kinds, lows, info_ref, q_ref, *refs
):
    kv_refs = refs[:pieces]
    out_ref, kv, stacked, top, acc = refs[pieces:]
    tile = pl.program_id(1)
    tile_q = q_ref.shape[0]
    factor = math.log2(math.e) / math.sqrt(HD)

    @pl.when(tile == 0)
    def _():
        at = 0
        for ref in kv_refs:
            kv[at : at + ref.shape[0], :] = ref[...]
            at += ref.shape[0]

    for head in range(per_group):
        stacked[pl.ds(head * tile_q, tile_q), :] = q_ref[:, head * HD : (head + 1) * HD]
    top[...] = jnp.full_like(top, NEG_FILL)
    acc[...] = jnp.zeros_like(acc)
    begin = info_ref[:, 0:1]
    stop = info_ref[:, 1:2]
    own = info_ref[:, 2:3]
    row = info_ref[:, 3:4]
    ones = jnp.ones((tile_k, HD), jnp.bfloat16)

    def block(slot, masked):
        start = pl.multiple_of(blocks[tile, slot] * tile_k, tile_k)
        key = kv[pl.ds(start, tile_k), 0:HD]
        value = jnp.concatenate([kv[pl.ds(start, tile_k), HD : 2 * HD], ones], axis=1)
        if masked:
            at = lows[blocks[tile, slot]] + lax.broadcasted_iota(jnp.int32, (tile_q, tile_k), 1)
            seen = (at <= row) & ((at >= own) | ((at >= begin) & (at < stop)))
            bias = jnp.where(seen, 0.0, NEG_FILL).astype(jnp.float32)
        chunk = min(CHUNK_HEADS, per_group)
        rows = chunk * tile_q
        for part in range(per_group // chunk):
            span = pl.ds(part * rows, rows)
            score = lax.dot_general(
                stacked[span, :], key, (((1,), (1,)), ((), ())),
                preferred_element_type=jnp.float32,
            )
            if masked:
                score = (score.reshape(chunk, tile_q, tile_k) + bias[None]).reshape(rows, tile_k)
            old = top[span, :]
            new = jnp.maximum(old, jnp.max(score, axis=1, keepdims=True))
            rescale = jnp.exp2((old - new) * factor)
            weight = jnp.exp2((score - jnp.tile(new, (1, tile_k // HD))) * factor)
            acc[span, :] = acc[span, :] * jnp.tile(rescale, (1, 2)) + jnp.dot(
                weight.astype(jnp.bfloat16), value, preferred_element_type=jnp.float32
            )
            top[span, :] = new

    def step(slot, carry):
        @pl.when(kinds[tile, slot] == 1)
        def _():
            block(slot, True)

        @pl.when(kinds[tile, slot] == 2)
        def _():
            block(slot, False)

        return carry

    lax.fori_loop(0, counts[tile], step, 0)
    live = row >= own
    for head in range(per_group):
        span = pl.ds(head * tile_q, tile_q)
        total = jnp.where(live, acc[span, HD : 2 * HD], 1.0)
        context = jnp.where(live, acc[span, 0:HD] / total, 0.0)
        out_ref[:, head * HD : (head + 1) * HD] = context.astype(out_ref.dtype)


def attend(queries, pieces, lows, info, key_heads, per_group):
    shard_rows = queries.shape[0]
    tile_q = min(TILE_Q, shard_rows)
    tile_k = TILE_K
    span_rows = sum(piece.shape[0] for piece in pieces)
    tiles = shard_rows // tile_q
    blocks = span_rows // tile_k
    low = lows[None, :]
    high = low + tile_k
    begin, stop, own, row = (info[:, c : c + 1] for c in range(4))
    end = jnp.minimum(stop, row + 1)
    touched = ((low < end) & (high > begin)) | ((low <= row) & (high > own))
    whole = ((low >= begin) & (high <= end)) | ((low >= own) & (high <= row + 1))
    touched = jnp.any(touched.reshape(tiles, tile_q, blocks), axis=1)
    whole = jnp.all(whole.reshape(tiles, tile_q, blocks), axis=1)
    kind = jnp.where(touched, jnp.where(whole, 2, 1), 0).astype(jnp.int32)
    counts = jnp.sum(touched.astype(jnp.int32), axis=1)
    place = jnp.cumsum(touched.astype(jnp.int32), axis=1) - 1
    slots = jnp.arange(blocks, dtype=jnp.int32)
    pick = touched[:, None, :] & (place[:, None, :] == slots[None, :, None])
    table = jnp.sum(jnp.where(pick, slots[None, None, :], 0), axis=2)
    kinds = jnp.sum(jnp.where(pick, kind[:, None, :], 0), axis=2)
    wide = per_group * HD
    kernel = functools.partial(attend_kernel, len(pieces), tile_k, per_group)
    flops = 4 * shard_rows * key_heads * wide * 1536
    return pl.pallas_call(
        kernel,
        out_shape=jax.ShapeDtypeStruct(queries.shape, jnp.bfloat16),
        grid_spec=pltpu.PrefetchScalarGridSpec(
            num_scalar_prefetch=4,
            grid=(key_heads, tiles),
            in_specs=[
                pl.BlockSpec((tile_q, info.shape[1]), lambda g, t, *_: (t, 0)),
                pl.BlockSpec((tile_q, wide), lambda g, t, *_: (t, g)),
            ]
            + [pl.BlockSpec((p.shape[0], 2 * HD), lambda g, t, *_: (0, g)) for p in pieces],
            out_specs=pl.BlockSpec((tile_q, wide), lambda g, t, *_: (t, g)),
            scratch_shapes=[
                pltpu.VMEM((span_rows, 2 * HD), jnp.bfloat16),
                pltpu.VMEM((per_group * tile_q, HD), jnp.bfloat16),
                pltpu.VMEM((per_group * tile_q, HD), jnp.float32),
                pltpu.VMEM((per_group * tile_q, 2 * HD), jnp.float32),
            ],
        ),
        compiler_params=pltpu.CompilerParams(vmem_limit_bytes=48 << 20),
        cost_estimate=pl.CostEstimate(
            flops=flops, bytes_accessed=4 * queries.size + 2 * span_rows * key_heads * 2 * HD,
            transcendentals=flops // (4 * HD),
        ),
        name="attend",
    )(counts, table, kinds, lows, info, queries, *pieces)


def pick_kernel(pages, index, source_ref, out_ref):
    def move(slot, carry):
        source = pl.multiple_of(index[slot] * PAGE, PAGE)
        target = pl.multiple_of(slot * PAGE, PAGE)
        out_ref[pl.ds(target, PAGE), :] = source_ref[pl.ds(source, PAGE), :]
        return carry

    lax.fori_loop(0, pages, move, 0)


def pick_pages(source, index):
    pages = index.shape[0]
    width = source.shape[1]
    return pl.pallas_call(
        functools.partial(pick_kernel, pages),
        out_shape=jax.ShapeDtypeStruct((pages * PAGE, width), source.dtype),
        grid_spec=pltpu.PrefetchScalarGridSpec(
            num_scalar_prefetch=1,
            grid=(1,),
            in_specs=[pl.BlockSpec(source.shape, lambda i, *_: (0, 0))],
            out_specs=pl.BlockSpec((pages * PAGE, width), lambda i, *_: (0, 0)),
        ),
        cost_estimate=pl.CostEstimate(
            flops=0, bytes_accessed=2 * (source.size + pages * PAGE * width), transcendentals=0
        ),
        name="pick",
    )(index, source)


def write_pages(keys_values, is_live, cache_page, own_index, axis_size):
    page_count = keys_values.shape[0] // PAGE
    capacity = (page_count + axis_size - 1) // axis_size
    slot_count = axis_size * capacity
    all_pages = cache_page.shape[0]
    owners = cache_page // page_count
    by_source = owners.reshape(axis_size, page_count)
    page_iota = jnp.arange(page_count, dtype=jnp.int32)
    earlier = page_iota[None, :] < page_iota[:, None]
    same_owner = by_source[:, :, None] == by_source[:, None, :]
    rank = jnp.sum((same_owner & earlier[None]).astype(jnp.int32), axis=2)
    my_owner = lax.dynamic_index_in_dim(by_source, own_index, 0, keepdims=False)
    my_rank = lax.dynamic_index_in_dim(rank, own_index, 0, keepdims=False)
    target_slot = my_owner * capacity + my_rank
    slot_iota = jnp.arange(slot_count, dtype=jnp.int32)
    send_page = jnp.sum(
        jnp.where(slot_iota[:, None] == target_slot[None, :], page_iota[None, :], 0), axis=1
    )
    masked = jnp.where(is_live[:, None], keys_values, jnp.zeros_like(keys_values))
    outgoing = pick_pages(masked, send_page)
    incoming = lax.all_to_all(outgoing, "req", split_axis=0, concat_axis=0, tiled=True)
    wanted = own_index * page_count + page_iota
    hits = cache_page[None, :] == wanted[:, None]
    page_slot = jnp.arange(all_pages, dtype=jnp.int32) // page_count * capacity + rank.reshape(-1)
    arrival = jnp.sum(jnp.where(hits, page_slot[None, :], 0), axis=1)
    return pick_pages(incoming, arrival)


def on_device(queries, keys_values, seg_ids, cache_page):
    shard_rows = queries.shape[0]
    key_heads = keys_values.shape[1] // (2 * HD)
    per_group = queries.shape[1] // HD // key_heads
    tokens = seg_ids.shape[0]
    own_index = lax.axis_index("req")
    axis_size = lax.axis_size("req")
    group = STREAM // shard_rows

    ids = jnp.arange(tokens // STREAM * (REQS + 1), dtype=jnp.int32)
    position = jnp.arange(tokens, dtype=jnp.int32)
    member = seg_ids[None, :] == ids[:, None]
    starts = jnp.min(jnp.where(member, position[None, :], tokens), axis=1)
    stops = jnp.max(jnp.where(member, position[None, :], -1), axis=1) + 1

    query_rows = own_index * shard_rows + jnp.arange(shard_rows, dtype=jnp.int32)
    query_seg = lax.dynamic_slice_in_dim(seg_ids, own_index * shard_rows, shard_rows)
    is_live = query_seg >= 0
    shared = query_seg // (REQS + 1) * (REQS + 1)
    far = 2 * tokens
    is_shared = shared[:, None] == ids[None, :]
    is_own = query_seg[:, None] == ids[None, :]
    begin = jnp.sum(jnp.where(is_shared, starts[None, :], 0), axis=1)
    stop = jnp.sum(jnp.where(is_shared, stops[None, :], 0), axis=1)
    own = jnp.sum(jnp.where(is_own, starts[None, :], 0), axis=1)
    begin = jnp.where(is_live, begin, far)
    stop = jnp.where(is_live, stop, 0)
    own = jnp.where(is_live, own, far)
    zero = jnp.zeros_like(own)
    info = jnp.stack([begin, stop, own, query_rows, zero, zero, zero, zero], axis=1)

    def answer(window, q, kv):
        pieces, lows = window(kv, group, own_index, tokens)
        return attend(q, pieces, lows, info, key_heads, per_group)

    prompt_ok = stops <= ids // (REQS + 1) * STREAM + LEAD + len(ROUNDS) * CHUNK
    request_ok = (stops - 1) // shard_rows - starts // shard_rows <= NEAR
    short = jnp.all(jnp.where(ids % (REQS + 1) == 0, prompt_ok, request_ok))
    if group == 8 and shard_rows == 2 * CHUNK:
        context = lax.cond(
            short,
            functools.partial(answer, short_window),
            functools.partial(answer, full_window),
            queries,
            keys_values,
        )
    else:
        context = answer(full_window, queries, keys_values)
    cache = write_pages(keys_values, is_live, cache_page, own_index, axis_size)
    return (context, cache)


def solution(mesh):
    return jax.shard_map(
        on_device,
        mesh=mesh,
        in_specs=(P("req", "head"), P("req", "head"), P(), P()),
        out_specs=(P("req", "head"), P("req", "head")),
        check_vma=False,
    )
```

```python
import functools
import math

import jax
import jax.numpy as jnp
from jax import lax
from jax.experimental import pallas as pl
from jax.experimental.pallas import tpu as pltpu
from jax.sharding import PartitionSpec as P

HD = 128
STREAM = 4096
REQS = 6
PAGE = 16

NEG_FILL = -1e30
TILE_Q = 128
TILE_K = 256
CHUNK_HEADS = 4
NEAR = 2
CHUNK = 256
LEAD = 256
ROUNDS = (
    ((0, 5, 0), (1, 6, 1), (2, 7, 2), (4, 8, 3), (3, 4, 1)),
    ((0, 6, 0), (1, 7, 1), (4, 5, 3), (3, 8, 2), (2, 4, 0)),
    ((0, 7, 0), (1, 8, 1), (2, 5, 2), (4, 6, 3), (3, 4, 2)),
    ((0, 8, 0), (1, 5, 1), (3, 6, 2), (4, 7, 3), (2, 3, 0)),
)


def from_before(keys_values, group, offset):
    count = lax.axis_size("req")
    pairs = [
        (base + a, base + a + offset)
        for base in range(0, count, group)
        for a in range(group)
        if a + offset <= group and base + a + offset < count
    ]
    return lax.ppermute(keys_values, "req", pairs) if pairs else jnp.zeros_like(keys_values)


def full_window(keys_values, group, own_index, tokens):
    shard_rows = keys_values.shape[0]
    pieces = [from_before(keys_values, group, offset) for offset in range(group, 0, -1)]
    blocks = (group + 1) * shard_rows // TILE_K
    first = (own_index - group) * shard_rows
    return pieces + [keys_values], first + jnp.arange(blocks, dtype=jnp.int32) * TILE_K


def short_window(keys_values, group, own_index, tokens):
    count = lax.axis_size("req")
    shard_rows = keys_values.shape[0]
    near = [from_before(keys_values, group, offset) for offset in range(NEAR, 0, -1)]
    pieces = near + [keys_values]
    held = jnp.concatenate(pieces, axis=0)
    blocks = held.shape[0] // TILE_K
    first = (own_index - NEAR) * shard_rows
    lows = [first + jnp.arange(blocks, dtype=jnp.int32) * TILE_K]
    place = own_index % group
    target_place = jnp.where(place == 0, group, place)
    base_row = (own_index - target_place) * shard_rows + LEAD
    for sends in ROUNDS:
        send = jnp.int32(0)
        take = jnp.int32(-1)
        for source, target, chunk in sends:
            row = LEAD + chunk * CHUNK - (source - NEAR) * shard_rows
            send = jnp.where(place == source, row, send)
            take = jnp.where(target_place == target, chunk, take)
        pairs = [
            (base + source, base + target)
            for base in range(0, count, group)
            for source, target, _ in sends
            if base + target < count
        ]
        pieces.append(
            lax.ppermute(lax.dynamic_slice_in_dim(held, send, CHUNK, 0), "req", pairs)
        )
        lows.append(jnp.where(take >= 0, base_row + take * CHUNK, 2 * tokens)[None])
    return pieces, jnp.concatenate(lows).astype(jnp.int32)


def attend_kernel(
    pieces, tile_k, per_group, counts, blocks, kinds, lows, info_ref, q_ref, *refs
):
    kv_refs = refs[:pieces]
    out_ref, kv, stacked, top, acc = refs[pieces:]
    tile = pl.program_id(1)
    tile_q = q_ref.shape[0]
    factor = math.log2(math.e) / math.sqrt(HD)

    @pl.when(tile == 0)
    def _():
        at = 0
        for ref in kv_refs:
            kv[at : at + ref.shape[0], :] = ref[...]
            at += ref.shape[0]

    for head in range(per_group):
        stacked[pl.ds(head * tile_q, tile_q), :] = q_ref[:, head * HD : (head + 1) * HD]
    top[...] = jnp.full_like(top, NEG_FILL)
    acc[...] = jnp.zeros_like(acc)
    begin = info_ref[:, 0:1]
    stop = info_ref[:, 1:2]
    own = info_ref[:, 2:3]
    row = info_ref[:, 3:4]
    ones = jnp.ones((tile_k, HD), jnp.bfloat16)

    def block(slot, masked):
        start = pl.multiple_of(blocks[tile, slot] * tile_k, tile_k)
        key = kv[pl.ds(start, tile_k), 0:HD]
        value = jnp.concatenate([kv[pl.ds(start, tile_k), HD : 2 * HD], ones], axis=1)
        if masked:
            at = lows[blocks[tile, slot]] + lax.broadcasted_iota(jnp.int32, (tile_q, tile_k), 1)
            seen = (at <= row) & ((at >= own) | ((at >= begin) & (at < stop)))
            bias = jnp.where(seen, 0.0, NEG_FILL).astype(jnp.float32)
        chunk = min(CHUNK_HEADS, per_group)
        rows = chunk * tile_q
        for part in range(per_group // chunk):
            span = pl.ds(part * rows, rows)
            score = lax.dot_general(
                stacked[span, :], key, (((1,), (1,)), ((), ())),
                preferred_element_type=jnp.float32,
            )
            if masked:
                score = (score.reshape(chunk, tile_q, tile_k) + bias[None]).reshape(rows, tile_k)
            old = top[span, :]
            new = jnp.maximum(old, jnp.max(score, axis=1, keepdims=True))
            rescale = jnp.exp2((old - new) * factor)
            weight = jnp.exp2((score - jnp.tile(new, (1, tile_k // HD))) * factor)
            acc[span, :] = acc[span, :] * jnp.tile(rescale, (1, 2)) + jnp.dot(
                weight.astype(jnp.bfloat16), value, preferred_element_type=jnp.float32
            )
            top[span, :] = new

    def step(slot, carry):
        @pl.when(kinds[tile, slot] == 1)
        def _():
            block(slot, True)

        @pl.when(kinds[tile, slot] == 2)
        def _():
            block(slot, False)

        return carry

    lax.fori_loop(0, counts[tile], step, 0)
    live = row >= own
    for head in range(per_group):
        span = pl.ds(head * tile_q, tile_q)
        total = jnp.where(live, acc[span, HD : 2 * HD], 1.0)
        context = jnp.where(live, acc[span, 0:HD] / total, 0.0)
        out_ref[:, head * HD : (head + 1) * HD] = context.astype(out_ref.dtype)


def attend(queries, pieces, lows, info, key_heads, per_group):
    shard_rows = queries.shape[0]
    tile_q = min(TILE_Q, shard_rows)
    tile_k = TILE_K
    span_rows = sum(piece.shape[0] for piece in pieces)
    tiles = shard_rows // tile_q
    blocks = span_rows // tile_k
    low = lows[None, :]
    high = low + tile_k
    begin, stop, own, row = (info[:, c : c + 1] for c in range(4))
    end = jnp.minimum(stop, row + 1)
    touched = ((low < end) & (high > begin)) | ((low <= row) & (high > own))
    whole = ((low >= begin) & (high <= end)) | ((low >= own) & (high <= row + 1))
    touched = jnp.any(touched.reshape(tiles, tile_q, blocks), axis=1)
    whole = jnp.all(whole.reshape(tiles, tile_q, blocks), axis=1)
    kind = jnp.where(touched, jnp.where(whole, 2, 1), 0).astype(jnp.int32)
    counts = jnp.sum(touched.astype(jnp.int32), axis=1)
    place = jnp.cumsum(touched.astype(jnp.int32), axis=1) - 1
    slots = jnp.arange(blocks, dtype=jnp.int32)
    pick = touched[:, None, :] & (place[:, None, :] == slots[None, :, None])
    table = jnp.sum(jnp.where(pick, slots[None, None, :], 0), axis=2)
    kinds = jnp.sum(jnp.where(pick, kind[:, None, :], 0), axis=2)
    wide = per_group * HD
    kernel = functools.partial(attend_kernel, len(pieces), tile_k, per_group)
    flops = 4 * shard_rows * key_heads * wide * 1536
    return pl.pallas_call(
        kernel,
        out_shape=jax.ShapeDtypeStruct(queries.shape, jnp.bfloat16),
        grid_spec=pltpu.PrefetchScalarGridSpec(
            num_scalar_prefetch=4,
            grid=(key_heads, tiles),
            in_specs=[
                pl.BlockSpec((tile_q, info.shape[1]), lambda g, t, *_: (t, 0)),
                pl.BlockSpec((tile_q, wide), lambda g, t, *_: (t, g)),
            ]
            + [pl.BlockSpec((p.shape[0], 2 * HD), lambda g, t, *_: (0, g)) for p in pieces],
            out_specs=pl.BlockSpec((tile_q, wide), lambda g, t, *_: (t, g)),
            scratch_shapes=[
                pltpu.VMEM((span_rows, 2 * HD), jnp.bfloat16),
                pltpu.VMEM((per_group * tile_q, HD), jnp.bfloat16),
                pltpu.VMEM((per_group * tile_q, HD), jnp.float32),
                pltpu.VMEM((per_group * tile_q, 2 * HD), jnp.float32),
            ],
        ),
        compiler_params=pltpu.CompilerParams(vmem_limit_bytes=48 << 20),
        cost_estimate=pl.CostEstimate(
            flops=flops, bytes_accessed=4 * queries.size + 2 * span_rows * key_heads * 2 * HD,
            transcendentals=flops // (4 * HD),
        ),
        name="attend",
    )(counts, table, kinds, lows, info, queries, *pieces)


def pick_kernel(pages, index, source_ref, out_ref):
    def move(slot, carry):
        source = pl.multiple_of(index[slot] * PAGE, PAGE)
        target = pl.multiple_of(slot * PAGE, PAGE)
        out_ref[pl.ds(target, PAGE), :] = source_ref[pl.ds(source, PAGE), :]
        return carry

    lax.fori_loop(0, pages, move, 0)


def pick_pages(source, index):
    pages = index.shape[0]
    width = source.shape[1]
    return pl.pallas_call(
        functools.partial(pick_kernel, pages),
        out_shape=jax.ShapeDtypeStruct((pages * PAGE, width), source.dtype),
        grid_spec=pltpu.PrefetchScalarGridSpec(
            num_scalar_prefetch=1,
            grid=(1,),
            in_specs=[pl.BlockSpec(source.shape, lambda i, *_: (0, 0))],
            out_specs=pl.BlockSpec((pages * PAGE, width), lambda i, *_: (0, 0)),
        ),
        cost_estimate=pl.CostEstimate(
            flops=0, bytes_accessed=2 * (source.size + pages * PAGE * width), transcendentals=0
        ),
        name="pick",
    )(index, source)


def write_pages(keys_values, is_live, cache_page, own_index, axis_size, pieces):
    page_count = keys_values.shape[0] // PAGE
    capacity = (page_count + axis_size - 1) // axis_size
    slot_count = axis_size * capacity
    all_pages = cache_page.shape[0]
    owners = cache_page // page_count
    by_source = owners.reshape(axis_size, page_count)
    page_iota = jnp.arange(page_count, dtype=jnp.int32)
    earlier = page_iota[None, :] < page_iota[:, None]
    same_owner = by_source[:, :, None] == by_source[:, None, :]
    rank = jnp.sum((same_owner & earlier[None]).astype(jnp.int32), axis=2)
    my_owner = lax.dynamic_index_in_dim(by_source, own_index, 0, keepdims=False)
    my_rank = lax.dynamic_index_in_dim(rank, own_index, 0, keepdims=False)
    target_slot = my_owner * capacity + my_rank
    slot_iota = jnp.arange(slot_count, dtype=jnp.int32)
    send_page = jnp.sum(
        jnp.where(slot_iota[:, None] == target_slot[None, :], page_iota[None, :], 0), axis=1
    )
    masked = jnp.where(is_live[:, None], keys_values, jnp.zeros_like(keys_values))
    outgoing = pick_pages(masked, send_page)
    outgoing, pieces = lax.optimization_barrier((outgoing, pieces))
    incoming = lax.all_to_all(outgoing, "req", split_axis=0, concat_axis=0, tiled=True)
    wanted = own_index * page_count + page_iota
    hits = cache_page[None, :] == wanted[:, None]
    page_slot = jnp.arange(all_pages, dtype=jnp.int32) // page_count * capacity + rank.reshape(-1)
    arrival = jnp.sum(jnp.where(hits, page_slot[None, :], 0), axis=1)
    return pick_pages(incoming, arrival), pieces


def on_device(queries, keys_values, seg_ids, cache_page):
    shard_rows = queries.shape[0]
    key_heads = keys_values.shape[1] // (2 * HD)
    per_group = queries.shape[1] // HD // key_heads
    tokens = seg_ids.shape[0]
    own_index = lax.axis_index("req")
    axis_size = lax.axis_size("req")
    group = STREAM // shard_rows

    ids = jnp.arange(tokens // STREAM * (REQS + 1), dtype=jnp.int32)
    position = jnp.arange(tokens, dtype=jnp.int32)
    member = seg_ids[None, :] == ids[:, None]
    starts = jnp.min(jnp.where(member, position[None, :], tokens), axis=1)
    stops = jnp.max(jnp.where(member, position[None, :], -1), axis=1) + 1

    query_rows = own_index * shard_rows + jnp.arange(shard_rows, dtype=jnp.int32)
    query_seg = lax.dynamic_slice_in_dim(seg_ids, own_index * shard_rows, shard_rows)
    is_live = query_seg >= 0
    shared = query_seg // (REQS + 1) * (REQS + 1)
    far = 2 * tokens
    is_shared = shared[:, None] == ids[None, :]
    is_own = query_seg[:, None] == ids[None, :]
    begin = jnp.sum(jnp.where(is_shared, starts[None, :], 0), axis=1)
    stop = jnp.sum(jnp.where(is_shared, stops[None, :], 0), axis=1)
    own = jnp.sum(jnp.where(is_own, starts[None, :], 0), axis=1)
    begin = jnp.where(is_live, begin, far)
    stop = jnp.where(is_live, stop, 0)
    own = jnp.where(is_live, own, far)
    zero = jnp.zeros_like(own)
    info = jnp.stack([begin, stop, own, query_rows, zero, zero, zero, zero], axis=1)

    def answer(window, q, kv):
        pieces, lows = window(kv, group, own_index, tokens)
        cache, pieces = write_pages(kv, is_live, cache_page, own_index, axis_size, pieces)
        return attend(q, pieces, lows, info, key_heads, per_group), cache

    prompt_ok = stops <= ids // (REQS + 1) * STREAM + LEAD + len(ROUNDS) * CHUNK
    request_ok = (stops - 1) // shard_rows - starts // shard_rows <= NEAR
    short = jnp.all(jnp.where(ids % (REQS + 1) == 0, prompt_ok, request_ok))
    if group == 8 and shard_rows == 2 * CHUNK:
        context, cache = lax.cond(
            short,
            functools.partial(answer, short_window),
            functools.partial(answer, full_window),
            queries,
            keys_values,
        )
    else:
        context, cache = answer(full_window, queries, keys_values)
    return (context, cache)


def solution(mesh):
    return jax.shard_map(
        on_device,
        mesh=mesh,
        in_specs=(P("req", "head"), P("req", "head"), P(), P()),
        out_specs=(P("req", "head"), P("req", "head")),
        check_vma=False,
    )
```

```python
import functools
import math

import jax
import jax.numpy as jnp
from jax import lax
from jax.experimental import pallas as pl
from jax.experimental.pallas import tpu as pltpu
from jax.sharding import PartitionSpec as P

HD = 128
STREAM = 4096
REQS = 6
PAGE = 16

NEG_FILL = -1e30
TILE_Q = 128
TILE_K = 256
CHUNK_HEADS = 4
NEAR = 2
CHUNK = 256
LEAD = 256
ROUNDS = (
    ((0, 5, 0), (1, 6, 1), (2, 7, 2), (4, 8, 3), (3, 4, 1)),
    ((0, 6, 0), (1, 7, 1), (4, 5, 3), (3, 8, 2), (2, 4, 0)),
    ((0, 7, 0), (1, 8, 1), (2, 5, 2), (4, 6, 3), (3, 4, 2)),
    ((0, 8, 0), (1, 5, 1), (3, 6, 2), (4, 7, 3), (2, 3, 0)),
)


def from_before(keys_values, group, offset):
    count = lax.axis_size("req")
    pairs = [
        (base + a, base + a + offset)
        for base in range(0, count, group)
        for a in range(group)
        if a + offset <= group and base + a + offset < count
    ]
    return lax.ppermute(keys_values, "req", pairs) if pairs else jnp.zeros_like(keys_values)


def full_window(keys_values, group, own_index, tokens):
    shard_rows = keys_values.shape[0]
    pieces = [from_before(keys_values, group, offset) for offset in range(group, 0, -1)]
    blocks = (group + 1) * shard_rows // TILE_K
    first = (own_index - group) * shard_rows
    return pieces + [keys_values], first + jnp.arange(blocks, dtype=jnp.int32) * TILE_K


def short_window(keys_values, group, own_index, tokens):
    count = lax.axis_size("req")
    shard_rows = keys_values.shape[0]
    near = [from_before(keys_values, group, offset) for offset in range(NEAR, 0, -1)]
    pieces = near + [keys_values]
    held = jnp.concatenate(pieces, axis=0)
    blocks = held.shape[0] // TILE_K
    first = (own_index - NEAR) * shard_rows
    lows = [first + jnp.arange(blocks, dtype=jnp.int32) * TILE_K]
    place = own_index % group
    target_place = jnp.where(place == 0, group, place)
    base_row = (own_index - target_place) * shard_rows + LEAD
    for sends in ROUNDS:
        send = jnp.int32(0)
        take = jnp.int32(-1)
        for source, target, chunk in sends:
            row = LEAD + chunk * CHUNK - (source - NEAR) * shard_rows
            send = jnp.where(place == source, row, send)
            take = jnp.where(target_place == target, chunk, take)
        pairs = [
            (base + source, base + target)
            for base in range(0, count, group)
            for source, target, _ in sends
            if base + target < count
        ]
        pieces.append(
            lax.ppermute(lax.dynamic_slice_in_dim(held, send, CHUNK, 0), "req", pairs)
        )
        lows.append(jnp.where(take >= 0, base_row + take * CHUNK, 2 * tokens)[None])
    return pieces, jnp.concatenate(lows).astype(jnp.int32)


def attend_kernel(
    pieces, tile_k, per_group, resume, finish, counts, blocks, kinds, lows, info_ref, q_ref, *refs
):
    kv_refs = refs[:pieces]
    refs = refs[pieces:]
    if resume:
        top_ref, acc_ref, refs = refs[0], refs[1], refs[2:]
    if finish:
        out_ref, kv, stacked, top, acc = refs
    else:
        top, acc, kv, stacked = refs
    tile = pl.program_id(1)
    tile_q = q_ref.shape[0]
    factor = math.log2(math.e) / math.sqrt(HD)

    @pl.when(tile == 0)
    def _():
        at = 0
        for ref in kv_refs:
            kv[at : at + ref.shape[0], :] = ref[...]
            at += ref.shape[0]

    for head in range(per_group):
        stacked[pl.ds(head * tile_q, tile_q), :] = q_ref[:, head * HD : (head + 1) * HD]
    if resume:
        top[...] = top_ref[...]
        acc[...] = acc_ref[...]
    else:
        top[...] = jnp.full_like(top, NEG_FILL)
        acc[...] = jnp.zeros_like(acc)
    begin = info_ref[:, 0:1]
    stop = info_ref[:, 1:2]
    own = info_ref[:, 2:3]
    row = info_ref[:, 3:4]
    ones = jnp.ones((tile_k, HD), jnp.bfloat16)

    def block(slot, masked):
        start = pl.multiple_of(blocks[tile, slot] * tile_k, tile_k)
        key = kv[pl.ds(start, tile_k), 0:HD]
        value = jnp.concatenate([kv[pl.ds(start, tile_k), HD : 2 * HD], ones], axis=1)
        if masked:
            at = lows[blocks[tile, slot]] + lax.broadcasted_iota(jnp.int32, (tile_q, tile_k), 1)
            seen = (at <= row) & ((at >= own) | ((at >= begin) & (at < stop)))
            bias = jnp.where(seen, 0.0, NEG_FILL).astype(jnp.float32)
        chunk = min(CHUNK_HEADS, per_group)
        rows = chunk * tile_q
        for part in range(per_group // chunk):
            span = pl.ds(part * rows, rows)
            score = lax.dot_general(
                stacked[span, :], key, (((1,), (1,)), ((), ())),
                preferred_element_type=jnp.float32,
            )
            if masked:
                score = (score.reshape(chunk, tile_q, tile_k) + bias[None]).reshape(rows, tile_k)
            old = top[span, :]
            new = jnp.maximum(old, jnp.max(score, axis=1, keepdims=True))
            rescale = jnp.exp2((old - new) * factor)
            weight = jnp.exp2((score - jnp.tile(new, (1, tile_k // HD))) * factor)
            acc[span, :] = acc[span, :] * jnp.tile(rescale, (1, 2)) + jnp.dot(
                weight.astype(jnp.bfloat16), value, preferred_element_type=jnp.float32
            )
            top[span, :] = new

    def step(slot, carry):
        @pl.when(kinds[tile, slot] == 1)
        def _():
            block(slot, True)

        @pl.when(kinds[tile, slot] == 2)
        def _():
            block(slot, False)

        return carry

    lax.fori_loop(0, counts[tile], step, 0)
    if not finish:
        return
    live = row >= own
    for head in range(per_group):
        span = pl.ds(head * tile_q, tile_q)
        total = jnp.where(live, acc[span, HD : 2 * HD], 1.0)
        context = jnp.where(live, acc[span, 0:HD] / total, 0.0)
        out_ref[:, head * HD : (head + 1) * HD] = context.astype(out_ref.dtype)


def attend(queries, pieces, lows, info, key_heads, per_group, state=(), finish=True):
    shard_rows = queries.shape[0]
    tile_q = min(TILE_Q, shard_rows)
    tile_k = TILE_K
    span_rows = sum(piece.shape[0] for piece in pieces)
    tiles = shard_rows // tile_q
    blocks = span_rows // tile_k
    low = lows[None, :]
    high = low + tile_k
    begin, stop, own, row = (info[:, c : c + 1] for c in range(4))
    end = jnp.minimum(stop, row + 1)
    touched = ((low < end) & (high > begin)) | ((low <= row) & (high > own))
    whole = ((low >= begin) & (high <= end)) | ((low >= own) & (high <= row + 1))
    touched = jnp.any(touched.reshape(tiles, tile_q, blocks), axis=1)
    whole = jnp.all(whole.reshape(tiles, tile_q, blocks), axis=1)
    kind = jnp.where(touched, jnp.where(whole, 2, 1), 0).astype(jnp.int32)
    counts = jnp.sum(touched.astype(jnp.int32), axis=1)
    place = jnp.cumsum(touched.astype(jnp.int32), axis=1) - 1
    slots = jnp.arange(blocks, dtype=jnp.int32)
    pick = touched[:, None, :] & (place[:, None, :] == slots[None, :, None])
    table = jnp.sum(jnp.where(pick, slots[None, None, :], 0), axis=2)
    kinds = jnp.sum(jnp.where(pick, kind[:, None, :], 0), axis=2)
    wide = per_group * HD
    kernel = functools.partial(attend_kernel, len(pieces), tile_k, per_group, bool(state), finish)
    rows = per_group * tile_q
    flops = 4 * shard_rows * key_heads * wide * 1536
    state_specs = [
        pl.BlockSpec((rows, cols), lambda g, t, *_: (g * tiles + t, 0)) for cols in (HD, 2 * HD)
    ]
    state_shapes = [
        jax.ShapeDtypeStruct((key_heads * tiles * rows, cols), jnp.float32)
        for cols in (HD, 2 * HD)
    ]
    state_scratch = [pltpu.VMEM((rows, cols), jnp.float32) for cols in (HD, 2 * HD)]
    context_spec = pl.BlockSpec((tile_q, wide), lambda g, t, *_: (t, g))
    context_shape = jax.ShapeDtypeStruct(queries.shape, jnp.bfloat16)
    return pl.pallas_call(
        kernel,
        out_shape=context_shape if finish else state_shapes,
        grid_spec=pltpu.PrefetchScalarGridSpec(
            num_scalar_prefetch=4,
            grid=(key_heads, tiles),
            in_specs=[
                pl.BlockSpec((tile_q, info.shape[1]), lambda g, t, *_: (t, 0)),
                pl.BlockSpec((tile_q, wide), lambda g, t, *_: (t, g)),
            ]
            + [pl.BlockSpec((p.shape[0], 2 * HD), lambda g, t, *_: (0, g)) for p in pieces]
            + (state_specs if state else []),
            out_specs=context_spec if finish else state_specs,
            scratch_shapes=[
                pltpu.VMEM((span_rows, 2 * HD), jnp.bfloat16),
                pltpu.VMEM((per_group * tile_q, HD), jnp.bfloat16),
            ]
            + (state_scratch if finish else []),
        ),
        compiler_params=pltpu.CompilerParams(vmem_limit_bytes=48 << 20),
        cost_estimate=pl.CostEstimate(
            flops=flops, bytes_accessed=4 * queries.size + 2 * span_rows * key_heads * 2 * HD,
            transcendentals=flops // (4 * HD),
        ),
        name="attend",
    )(counts, table, kinds, lows, info, queries, *pieces, *state)


def pick_kernel(pages, index, source_ref, out_ref):
    def move(slot, carry):
        source = pl.multiple_of(index[slot] * PAGE, PAGE)
        target = pl.multiple_of(slot * PAGE, PAGE)
        out_ref[pl.ds(target, PAGE), :] = source_ref[pl.ds(source, PAGE), :]
        return carry

    lax.fori_loop(0, pages, move, 0)


def pick_pages(source, index):
    pages = index.shape[0]
    width = source.shape[1]
    return pl.pallas_call(
        functools.partial(pick_kernel, pages),
        out_shape=jax.ShapeDtypeStruct((pages * PAGE, width), source.dtype),
        grid_spec=pltpu.PrefetchScalarGridSpec(
            num_scalar_prefetch=1,
            grid=(1,),
            in_specs=[pl.BlockSpec(source.shape, lambda i, *_: (0, 0))],
            out_specs=pl.BlockSpec((pages * PAGE, width), lambda i, *_: (0, 0)),
        ),
        cost_estimate=pl.CostEstimate(
            flops=0, bytes_accessed=2 * (source.size + pages * PAGE * width), transcendentals=0
        ),
        name="pick",
    )(index, source)


def write_pages(keys_values, is_live, cache_page, own_index, axis_size, pieces):
    page_count = keys_values.shape[0] // PAGE
    capacity = (page_count + axis_size - 1) // axis_size
    slot_count = axis_size * capacity
    all_pages = cache_page.shape[0]
    owners = cache_page // page_count
    by_source = owners.reshape(axis_size, page_count)
    page_iota = jnp.arange(page_count, dtype=jnp.int32)
    earlier = page_iota[None, :] < page_iota[:, None]
    same_owner = by_source[:, :, None] == by_source[:, None, :]
    rank = jnp.sum((same_owner & earlier[None]).astype(jnp.int32), axis=2)
    my_owner = lax.dynamic_index_in_dim(by_source, own_index, 0, keepdims=False)
    my_rank = lax.dynamic_index_in_dim(rank, own_index, 0, keepdims=False)
    target_slot = my_owner * capacity + my_rank
    slot_iota = jnp.arange(slot_count, dtype=jnp.int32)
    send_page = jnp.sum(
        jnp.where(slot_iota[:, None] == target_slot[None, :], page_iota[None, :], 0), axis=1
    )
    masked = jnp.where(is_live[:, None], keys_values, jnp.zeros_like(keys_values))
    outgoing = pick_pages(masked, send_page)
    outgoing, pieces = lax.optimization_barrier((outgoing, pieces))
    incoming = lax.all_to_all(outgoing, "req", split_axis=0, concat_axis=0, tiled=True)
    wanted = own_index * page_count + page_iota
    hits = cache_page[None, :] == wanted[:, None]
    page_slot = jnp.arange(all_pages, dtype=jnp.int32) // page_count * capacity + rank.reshape(-1)
    arrival = jnp.sum(jnp.where(hits, page_slot[None, :], 0), axis=1)
    return pick_pages(incoming, arrival), pieces


def on_device(queries, keys_values, seg_ids, cache_page):
    shard_rows = queries.shape[0]
    key_heads = keys_values.shape[1] // (2 * HD)
    per_group = queries.shape[1] // HD // key_heads
    tokens = seg_ids.shape[0]
    own_index = lax.axis_index("req")
    axis_size = lax.axis_size("req")
    group = STREAM // shard_rows

    ids = jnp.arange(tokens // STREAM * (REQS + 1), dtype=jnp.int32)
    position = jnp.arange(tokens, dtype=jnp.int32)
    member = seg_ids[None, :] == ids[:, None]
    starts = jnp.min(jnp.where(member, position[None, :], tokens), axis=1)
    stops = jnp.max(jnp.where(member, position[None, :], -1), axis=1) + 1

    query_rows = own_index * shard_rows + jnp.arange(shard_rows, dtype=jnp.int32)
    query_seg = lax.dynamic_slice_in_dim(seg_ids, own_index * shard_rows, shard_rows)
    is_live = query_seg >= 0
    shared = query_seg // (REQS + 1) * (REQS + 1)
    far = 2 * tokens
    is_shared = shared[:, None] == ids[None, :]
    is_own = query_seg[:, None] == ids[None, :]
    begin = jnp.sum(jnp.where(is_shared, starts[None, :], 0), axis=1)
    stop = jnp.sum(jnp.where(is_shared, stops[None, :], 0), axis=1)
    own = jnp.sum(jnp.where(is_own, starts[None, :], 0), axis=1)
    begin = jnp.where(is_live, begin, far)
    stop = jnp.where(is_live, stop, 0)
    own = jnp.where(is_live, own, far)
    zero = jnp.zeros_like(own)
    info = jnp.stack([begin, stop, own, query_rows, zero, zero, zero, zero], axis=1)

    def answer(window, q, kv):
        pieces, lows = window(kv, group, own_index, tokens)
        if window is full_window:
            cache, pieces = write_pages(kv, is_live, cache_page, own_index, axis_size, pieces)
            return attend(q, pieces, lows, info, key_heads, per_group), cache
        held = (NEAR + 1) * shard_rows // TILE_K
        near, far = pieces[: NEAR + 1], pieces[NEAR + 1 :]
        state = attend(q, near, lows[:held], info, key_heads, per_group, finish=False)
        cache, (far, state) = write_pages(
            kv, is_live, cache_page, own_index, axis_size, (far, tuple(state))
        )
        context = attend(q, far, lows[held:], info, key_heads, per_group, state=state)
        return context, cache

    prompt_ok = stops <= ids // (REQS + 1) * STREAM + LEAD + len(ROUNDS) * CHUNK
    request_ok = (stops - 1) // shard_rows - starts // shard_rows <= NEAR
    short = jnp.all(jnp.where(ids % (REQS + 1) == 0, prompt_ok, request_ok))
    if group == 8 and shard_rows == 2 * CHUNK:
        context, cache = lax.cond(
            short,
            functools.partial(answer, short_window),
            functools.partial(answer, full_window),
            queries,
            keys_values,
        )
    else:
        context, cache = answer(full_window, queries, keys_values)
    return (context, cache)


def solution(mesh):
    return jax.shard_map(
        on_device,
        mesh=mesh,
        in_specs=(P("req", "head"), P("req", "head"), P(), P()),
        out_specs=(P("req", "head"), P("req", "head")),
        check_vma=False,
    )
```
